32 devices in a mesh: layer: 8 (over z, x), batch: 4 (over y, core).
Axes of the slice: x: 2, y: 2, z: 4, core: 2. Of those that a mesh axis runs over, the one named last changes fastest.
Arguments:
- inputs: float32 [4, 8, 8, 8, 128], P('batch'), parts along dimension 0, may hold values from -6 to 6
- guess_states: float32 [32, 4, 8, 8, 8, 128], P('layer', 'batch'), parts along dimension 1, may hold values from -6 to 6
- kernels: bfloat16 [32, 3, 3, 3, 128, 128], P('layer'), may hold values from -0.109375 to 0.109375
- biases: float32 [32, 128], P('layer'), may hold values from -4 to 4
Outputs:
- states: float32 [32, 4, 8, 8, 8, 128], P('layer', 'batch'), parts along dimension 1
- coarse_residual: float32 [8, 4, 8, 8, 8, 128], P('layer', 'batch'), parts along dimension 1
The draws below stay inside these ranges and needn't reach their ends.
There are 4 independent parts, one for each index of `batch`. The reference program is written for one: setup_inputs(seed, part) draws one part's arguments, and reference() takes and returns one part's arrays. A program takes and returns all parts, laid end to end along the dimension named above; an argument that names none is the same for every part. Nothing has to cross between parts.
All inputs are finite; a program needn't handle non-finite values.
Results may differ from the reference program's by a relative error of at most 0.0008.
Values may be sent and summed in bfloat16 or wider, within the bound.
A program may use at most 128 MiB of HBM per device.

```python
import jax
import jax.numpy as jnp
from jax import lax

CHANNELS = 128
VX = 8
VY = 8
VZ = 8
CLIPS = 1
SECT = 4
COARSEN = 4
LAYERS = 32
N_LAYER = 8


def level_of(stream_key, shape, cuts, low, high):
    def one(dim, blocks):
        steps = jax.random.uniform(jax.random.fold_in(jax.random.fold_in(stream_key, 6), dim), (blocks,), jnp.float32, low / len(cuts), high / len(cuts))
        return jnp.repeat(jnp.exp(steps), shape[dim] // blocks).reshape((-1,) + (1,) * (len(shape) - dim - 1))

    level = one(*cuts[0])
    for cut in cuts[1:]:
        level = level * one(*cut)
    return level


def bell_draw(stream_key, extent, scale, bound, shards=(), held_as=jnp.bfloat16):
    drawn = jax.random.normal(stream_key, extent, jnp.float32) * scale
    if len(shards) > 0:
        drawn = level_of(stream_key, extent, shards, -0.22, 0.18) * drawn
    return jnp.clip(drawn, min=-bound, max=bound).astype(held_as)


def setup_inputs(seed: int = 0, part: int = 0) -> dict:
    key_list = jax.random.split(jax.random.key(seed), 5)
    part_keys = jax.random.split(jax.random.fold_in(key_list[4], part), 5)
    inputs = bell_draw(part_keys[0], (CLIPS, VX, VY, VZ, CHANNELS), 1.0, 6.0, (), jnp.float32)
    guess_states = bell_draw(part_keys[1], (LAYERS, CLIPS, VX, VY, VZ, CHANNELS), 1.0, 6.0, ((0, 8),), jnp.float32)
    kernels = bell_draw(key_list[2], (LAYERS, 3, 3, 3, CHANNELS, CHANNELS), (27 * CHANNELS) ** -0.5, 0.109375, ((0, 8),))
    biases = bell_draw(key_list[3], (LAYERS, CHANNELS), 1.0, 4.0, ((0, 8),), jnp.float32)
    return dict(inputs=inputs, guess_states=guess_states, kernels=kernels, biases=biases)


def advance(state, kernel, offset_row, step_size):
    squashed = lax.optimization_barrier(jnp.tanh(state).astype(jnp.bfloat16)).astype(jnp.float32)
    count, size_x, size_y, size_z, width = state.shape
    padded = jnp.pad(squashed, ((0, 0), (1, 1), (1, 1), (1, 1), (0, 0)))
    pieces = []
    for shift_a in range(3):
        for shift_b in range(3):
            for shift_d in range(3):
                pieces.append(padded[:, shift_a:shift_a + size_x, shift_b:shift_b + size_y, shift_d:shift_d + size_z, :])
    columns = jnp.concatenate(pieces, -1).reshape((-1, 27 * width))
    matrix = kernel.astype(jnp.float32).reshape((27 * width, kernel.shape[-1]))
    mixed = jnp.dot(columns, matrix, precision=lax.Precision.HIGHEST, preferred_element_type=jnp.float32)
    mixed = mixed.reshape((count, size_x, size_y, size_z, kernel.shape[-1]))
    return state + step_size * (mixed + offset_row)


def reference(inputs, guess_states, kernels, biases):
    sections = N_LAYER
    depth = SECT
    groups = sections // COARSEN
    fine_size = 2.0 / (SECT * N_LAYER)
    coarse_size = depth * fine_size
    top_size = COARSEN * coarse_size
    stepper = jax.vmap(advance, in_axes=(0, 0, 0, None))
    tail = guess_states.shape[1:]
    states = guess_states.reshape((sections, depth) + tail)
    kernel_grid = kernels.reshape((sections, depth) + kernels.shape[1:])
    bias_grid = biases.reshape((sections, depth, biases.shape[-1]))

    def heads_of(current):
        return jnp.concatenate([inputs[None], current[:-1, -1]], 0)

    def relax_fine(current):
        chain_rows = [heads_of(current)]
        for layer_row in range(1, depth):
            chain_rows.append(stepper(chain_rows[-1], kernel_grid[:, layer_row - 1], bias_grid[:, layer_row - 1], fine_size))
        return jnp.stack(chain_rows[1:] + [current[:, -1]], 1)

    def settle_fine(current):
        corner = stepper(current[:, -2], kernel_grid[:, -1], bias_grid[:, -1], fine_size)
        return current.at[:, -1].set(corner)

    states = relax_fine(settle_fine(relax_fine(states)))
    heads = heads_of(states)
    fine_defect = stepper(states[:, -2], kernel_grid[:, -1], bias_grid[:, -1], fine_size) - stepper(heads, kernel_grid[:, 0], bias_grid[:, 0], coarse_size)

    coarse_values = states[:, -1].reshape((groups, COARSEN) + tail)
    coarse_defect = fine_defect.reshape((groups, COARSEN) + tail)
    coarse_kernels = kernel_grid[:, 0].reshape((groups, COARSEN) + kernels.shape[1:])
    coarse_biases = bias_grid[:, 0].reshape((groups, COARSEN, biases.shape[-1]))

    def coarse_heads(current):
        return jnp.concatenate([inputs[None], current[:-1, -1]], 0)

    def relax_coarse(current):
        chain_rows = [coarse_heads(current)]
        for turn in range(COARSEN - 1):
            chain_rows.append(stepper(chain_rows[-1], coarse_kernels[:, turn], coarse_biases[:, turn], coarse_size) + coarse_defect[:, turn])
        return jnp.stack(chain_rows[1:] + [current[:, -1]], 1)

    def settle_coarse(current):
        corner = stepper(current[:, -2], coarse_kernels[:, -1], coarse_biases[:, -1], coarse_size) + coarse_defect[:, -1]
        return current.at[:, -1].set(corner)

    coarse_values = relax_coarse(settle_coarse(relax_coarse(coarse_values)))
    group_heads = coarse_heads(coarse_values)
    flat_values = coarse_values.reshape((sections,) + tail)
    flat_heads = jnp.concatenate([inputs[None], flat_values[:-1]], 0)
    corner_all = stepper(flat_heads, kernel_grid[:, 0], bias_grid[:, 0], coarse_size) + fine_defect
    coarse_residual = corner_all - flat_values
    corner_owner = corner_all.reshape((groups, COARSEN) + tail)[:, -1]
    level_defect = corner_owner - stepper(group_heads, coarse_kernels[:, -1], coarse_biases[:, -1], top_size)

    level_two = inputs
    solved = []
    for turn in range(groups):
        level_two = advance(level_two, coarse_kernels[turn, -1], coarse_biases[turn, -1], top_size) + level_defect[turn]
        solved.append(level_two)
    coarse_values = coarse_values.at[:, -1].set(jnp.stack(solved, 0))
    coarse_values = relax_coarse(coarse_values)

    states = states.at[:, -1].set(coarse_values.reshape((sections,) + tail))
    states = relax_fine(states)
    return states.reshape(guess_states.shape), coarse_residual
```

```python
import jax
import jax.numpy as jnp
from jax import lax
from jax.experimental import pallas as pl
from jax.experimental.pallas import tpu as pltpu
from jax.sharding import PartitionSpec as P

COARSEN = 4
TAPS = 3
MESH = pl.DeviceIdType.MESH


def cycle_kernel(sections, inputs_ref, guess_ref, kern_ref, bias_ref, states_ref, residual_ref,
                 fine_w, lead_w, patches, cur, head, head_mix, first_head, next_head, corner_out,
                 start_in, group_in, top_head, top_rhs, defects, top_in, top_out,
                 load_sem, lead_sem, hop_send, hop_recv, w_send, w_recv, sib_send, sib_recv,
                 head_send, head_recv, g_send, g_recv, jump_send, jump_recv):
    depth = guess_ref.shape[0]
    size_x, size_y, size_z, width = inputs_ref.shape
    groups = sections // COARSEN
    fine_size = 2.0 / (depth * sections)
    coarse_size = depth * fine_size
    top_size = COARSEN * coarse_size
    rows = TAPS * TAPS * width
    half_rows = rows // 2
    me = lax.axis_index("layer")
    part = lax.axis_index("batch")
    pos = lax.rem(me, COARSEN)
    group = me // COARSEN
    core = lax.rem(part, 2)
    sibling = part + 1 - 2 * core
    is_first = me == 0
    has_next = me < sections - 1
    has_group_before = group > 0
    has_group_after = group < groups - 1

    def peer(rel):
        return (group * COARSEN + lax.rem(pos + rel, COARSEN), part)

    def slot_from(rel):
        return lax.rem(pos + COARSEN - rel, COARSEN)

    def fine_load(layer, tap):
        return pltpu.make_async_copy(
            kern_ref.at[layer, tap],
            fine_w.at[layer, :, pl.ds(tap * width, width)],
            load_sem.at[layer, tap],
        )

    def lead_load(tap):
        return pltpu.make_async_copy(
            kern_ref.at[0, tap],
            lead_w.at[pos, :, pl.ds(tap * width, width)],
            lead_sem.at[tap],
        )

    for layer in range(depth):
        for tap in range(TAPS):
            fine_load(layer, tap).start()
    for tap in range(TAPS):
        lead_load(tap).start()

    barrier = pltpu.get_barrier_semaphore()

    def greet(device):
        pl.semaphore_signal(barrier, inc=1, device_id=device, device_id_type=MESH)

    partners = [(has_next, (me + 1, part)), (me > 0, (me - 1, part)),
                (has_group_after, (me + COARSEN, part)), (has_group_before, (me - COARSEN, part))]
    for there, device in partners:
        pl.when(there)(lambda device=device: greet(device))
    for rel in range(1, COARSEN):
        greet(peer(rel))
    greet((me, sibling))
    greetings = sum(jnp.where(there, 1, 0) for there, _ in partners)
    pl.semaphore_wait(barrier, COARSEN + greetings)

    def hop(index, source, target):
        return pltpu.make_async_remote_copy(
            src_ref=source, dst_ref=target, send_sem=hop_send.at[index], recv_sem=hop_recv.at[index],
            device_id=(me + 1, part), device_id_type=MESH)

    first_hop = hop(0, guess_ref.at[depth - 1, 0], first_head)
    second_hop = hop(1, corner_out, next_head)
    pl.when(has_next)(first_hop.start)

    def half(which):
        return pl.ds(pl.multiple_of(which * half_rows, 16), half_rows)

    def w_copy(rel):
        return pltpu.make_async_remote_copy(
            src_ref=lead_w.at[pos, half(core)], dst_ref=lead_w.at[pos, half(core)],
            send_sem=w_send.at[rel], recv_sem=w_recv.at[rel],
            device_id=peer(rel), device_id_type=MESH)

    def w_arrival(rel):
        return pltpu.make_async_remote_copy(
            src_ref=lead_w.at[slot_from(rel), half(core)], dst_ref=lead_w.at[slot_from(rel), half(core)],
            send_sem=w_send.at[rel], recv_sem=w_recv.at[rel],
            device_id=peer(rel), device_id_type=MESH)

    def sib_copy(rel, which):
        return pltpu.make_async_remote_copy(
            src_ref=lead_w.at[slot_from(rel), half(which)], dst_ref=lead_w.at[slot_from(rel), half(which)],
            send_sem=sib_send.at[rel], recv_sem=sib_recv.at[rel],
            device_id=(me, sibling), device_id_type=MESH)

    for tap in range(TAPS):
        lead_load(tap).wait()
    for rel in range(1, COARSEN):
        w_copy(rel).start()

    z_index = lax.broadcasted_iota(jnp.int32, (size_x * size_y, size_z, width), 1)

    def mix(state, weights):
        squashed = jnp.tanh(state).reshape(size_x * size_y, size_z, width)
        below = jnp.where(z_index == 0, 0.0, pltpu.roll(squashed, 1, 1))
        above = jnp.where(z_index == size_z - 1, 0.0, pltpu.roll(squashed, size_z - 1, 1))
        edge = jnp.zeros((size_x, 1, size_z, width), jnp.float32)
        span = size_y * size_z
        for tap_z, shifted in enumerate((below, squashed, above)):
            shifted = shifted.reshape(size_x, size_y, size_z, width)
            even = shifted.reshape(size_x, span, width).astype(jnp.bfloat16)
            odd = jnp.concatenate([edge, shifted, edge], 1)
            odd = odd.reshape(size_x, span + 2 * size_z, width).astype(jnp.bfloat16)
            for tap_y, block in enumerate((odd[:, :span], even, odd[:, 2 * size_z:])):
                column = (tap_y * TAPS + tap_z) * width
                patches[:, :, column:column + width] = block
        left = patches[...].reshape(size_x * span, rows)
        product = jnp.dot(left, weights[...], preferred_element_type=jnp.float32)
        product = product.reshape(size_x, size_y, size_z, TAPS * width)
        plane = jnp.zeros((1, size_y, size_z, width), jnp.float32)
        total = product[..., width:2 * width]
        total = total + jnp.concatenate([plane, product[:-1, :, :, :width]], 0)
        return total + jnp.concatenate([product[1:, :, :, 2 * width:], plane], 0)

    def fine_step(layer):
        state = cur[...]
        mixed = mix(state, fine_w.at[layer])
        return state, mixed, state + fine_size * (mixed + bias_ref[layer])

    pl.when(has_next)(first_hop.wait_send)
    pl.when(me > 0)(first_hop.wait_recv)
    cur[...] = jnp.where(is_first, inputs_ref[...], first_head[...])

    for layer in range(depth):
        for tap in range(TAPS):
            fine_load(layer, tap).wait()

    def sweep_one(layer, carry):
        cur[...] = fine_step(layer)[2]
        return carry

    lax.fori_loop(0, depth, sweep_one, 0)
    corner_out[...] = cur[...]
    pl.when(has_next)(second_hop.start)

    for rel in range(1, COARSEN):
        w_arrival(rel).wait_recv()
        sib_copy(rel, core).start()

    pl.when(has_next)(second_hop.wait_send)
    pl.when(me > 0)(second_hop.wait_recv)

    def head_copy(rel):
        return pltpu.make_async_remote_copy(
            src_ref=next_head, dst_ref=group_in, send_sem=head_send.at[rel], recv_sem=head_recv,
            device_id=peer(rel), device_id_type=MESH)

    leads_group = jnp.logical_and(pos == 0, has_group_before)
    follows = jnp.logical_and(pos > 0, has_group_before)
    for rel in range(1, COARSEN):
        pl.when(leads_group)(head_copy(rel).start)
    head[...] = jnp.where(is_first, inputs_ref[...], next_head[...])
    cur[...] = head[...]

    def sweep_two(layer, carry):
        _, mixed, after = fine_step(layer)

        @pl.when(layer == 0)
        def _():
            head_mix[...] = mixed

        cur[...] = after
        return carry

    lax.fori_loop(0, depth, sweep_two, 0)
    defects[pos] = cur[...] - head[...] - coarse_size * head_mix[...]

    def g_copy(rel):
        return pltpu.make_async_remote_copy(
            src_ref=defects.at[pos], dst_ref=defects.at[pos],
            send_sem=g_send.at[rel], recv_sem=g_recv.at[rel], device_id=peer(rel), device_id_type=MESH)

    def g_arrival(rel):
        return pltpu.make_async_remote_copy(
            src_ref=defects.at[slot_from(rel)], dst_ref=defects.at[slot_from(rel)],
            send_sem=g_send.at[rel], recv_sem=g_recv.at[rel], device_id=peer(rel), device_id_type=MESH)

    for rel in range(1, COARSEN):
        g_copy(rel).start()

    pl.when(follows)(head_copy(1).wait_recv)

    @pl.when(group == 0)
    def _():
        cur[...] = inputs_ref[...]

    @pl.when(leads_group)
    def _():
        cur[...] = next_head[...]

    @pl.when(follows)
    def _():
        cur[...] = group_in[...]

    for rel in range(1, COARSEN):
        sib_copy(rel, 1 - core).wait_recv()
        g_arrival(rel).wait_recv()

    def chain(count):
        def step(turn, carry):
            state = cur[...]
            mixed = mix(state, lead_w.at[turn])

            @pl.when(turn == pos)
            def _():
                head[...] = state
                head_mix[...] = mixed

            after = state + coarse_size * mixed + defects[turn]
            cur[...] = after
            return carry

        lax.fori_loop(0, COARSEN, step, 0)

    def jump(index, source, target):
        return pltpu.make_async_remote_copy(
            src_ref=source, dst_ref=target, send_sem=jump_send.at[index], recv_sem=jump_recv.at[index],
            device_id=(me + COARSEN, part), device_id_type=MESH)

    chain(COARSEN)
    corner_out[...] = cur[...]
    relaxed = jump(0, corner_out, start_in)
    pl.when(has_group_after)(relaxed.start)
    pl.when(has_group_after)(relaxed.wait_send)
    pl.when(has_group_before)(relaxed.wait_recv)
    group_in_first = group == 0

    def started():
        return jnp.where(group_in_first, inputs_ref[...], start_in[...])

    cur[...] = started()
    chain(COARSEN)
    is_owner = pos == COARSEN - 1
    corner = cur[...]
    residual_ref[0, 0] = jnp.where(is_owner, corner - corner_out[...], corner - corner)

    top_w = lead_w.at[COARSEN - 1]
    top_rhs[...] = corner - started() - top_size * mix(started(), top_w)
    solved = jump(1, top_out, top_in)
    pl.when(has_group_before)(solved.wait_recv)
    top_head[...] = jnp.where(group_in_first, inputs_ref[...], top_in[...])
    top_out[...] = top_head[...] + top_size * mix(top_head[...], top_w) + top_rhs[...]
    pl.when(has_group_after)(solved.start)

    cur[...] = top_head[...]
    chain(COARSEN)

    first = head[...] + coarse_size * head_mix[...] + defects[pos]
    states_ref[depth - 1, 0] = jnp.where(is_owner, top_out[...], first)
    cur[...] = head[...] + fine_size * (head_mix[...] + bias_ref[0])
    states_ref[0, 0] = cur[...]

    def last_sweep(layer, carry):
        after = fine_step(layer)[2]
        cur[...] = after
        states_ref[layer, 0] = after
        return carry

    lax.fori_loop(1, depth - 1, last_sweep, 0)

    for rel in range(1, COARSEN):
        w_copy(rel).wait_send()
        sib_copy(rel, core).wait_send()
        g_copy(rel).wait_send()
        pl.when(leads_group)(head_copy(rel).wait_send)
    pl.when(has_group_after)(solved.wait_send)


def shards(inputs, guess_states, kernels, biases):
    sections = lax.axis_size("layer")
    depth = guess_states.shape[0]
    state = inputs.shape[1:]
    width = state[-1]
    rows = TAPS * TAPS * width
    vmem = pl.BlockSpec(memory_space=pltpu.VMEM)
    anywhere = pl.BlockSpec(memory_space=pl.ANY)
    kernel_rows = kernels.reshape(depth, TAPS, rows, width)
    bias_rows = biases.reshape(depth, 1, 1, width)
    f32_state = pltpu.VMEM(state, jnp.float32)
    dma = pltpu.SemaphoreType.DMA

    def body(*refs):
        cycle_kernel(sections, *refs)

    return tuple(pl.pallas_call(
        body,
        name="mgrit_cycle",
        out_shape=(
            jax.ShapeDtypeStruct(guess_states.shape, jnp.float32),
            jax.ShapeDtypeStruct((1,) + guess_states.shape[1:], jnp.float32),
        ),
        in_specs=[vmem, anywhere, anywhere, vmem],
        out_specs=(vmem, vmem),
        scratch_shapes=[
            pltpu.VMEM((depth, rows, TAPS * width), jnp.bfloat16),
            pltpu.VMEM((COARSEN, rows, TAPS * width), jnp.bfloat16),
            pltpu.VMEM((state[0], state[1] * state[2], rows), jnp.bfloat16),
            f32_state, f32_state, f32_state, f32_state, f32_state, f32_state,
            f32_state, f32_state, f32_state, f32_state,
            pltpu.VMEM((COARSEN,) + state, jnp.float32),
            f32_state, f32_state,
            dma((depth, TAPS)), dma((TAPS,)), dma((2,)), dma((2,)),
            dma((COARSEN,)), dma((COARSEN,)), dma((COARSEN,)), dma((COARSEN,)),
            dma((COARSEN,)), dma, dma((COARSEN,)), dma((COARSEN,)), dma((2,)), dma((2,)),
        ],
        compiler_params=pltpu.CompilerParams(
            collective_id=0, has_side_effects=True, vmem_limit_bytes=48 * 1024 * 1024),
    )(inputs.reshape(state), guess_states, kernel_rows, bias_rows))


def solution(mesh):
    return jax.shard_map(
        shards,
        mesh=mesh,
        in_specs=(
            P("batch", None, None, None, None),
            P("layer", "batch", None, None, None, None),
            P("layer", None, None, None, None, None),
            P("layer", None),
        ),
        out_specs=(
            P("layer", "batch", None, None, None, None),
            P("layer", "batch", None, None, None, None),
        ),
        check_vma=False,
    )
```

```python
import jax
import jax.numpy as jnp
from jax import lax
from jax.experimental import pallas as pl
from jax.experimental.pallas import tpu as pltpu
from jax.sharding import PartitionSpec as P

COARSEN = 4
TAPS = 3
MESH = pl.DeviceIdType.MESH


def cycle_kernel(sections, inputs_ref, guess_ref, kern_ref, bias_ref, states_ref, residual_ref,
                 fine_w, lead_w, patches, cur, head, head_mix, first_head, next_head, corner_out,
                 start_in, group_in, top_head, top_rhs, defects, top_in, top_out,
                 load_sem, lead_sem, hop_send, hop_recv, w_send, w_recv, sib_send, sib_recv,
                 head_send, head_recv, g_send, g_recv, jump_send, jump_recv):
    depth = guess_ref.shape[0]
    size_x, size_y, size_z, width = inputs_ref.shape
    groups = sections // COARSEN
    fine_size = 2.0 / (depth * sections)
    coarse_size = depth * fine_size
    top_size = COARSEN * coarse_size
    rows = TAPS * TAPS * width
    half_rows = rows // 2
    me = lax.axis_index("layer")
    part = lax.axis_index("batch")
    pos = lax.rem(me, COARSEN)
    group = me // COARSEN
    core = lax.rem(part, 2)
    sibling = part + 1 - 2 * core
    is_first = me == 0
    has_next = me < sections - 1
    has_group_before = group > 0
    has_group_after = group < groups - 1
    span_low = COARSEN // 2
    is_upper = pos >= span_low

    def peer(rel):
        return (group * COARSEN + lax.rem(pos + rel, COARSEN), part)

    def wanted(source, target):
        return jnp.logical_or(target >= span_low, target > source)

    def gives(rel):
        return wanted(pos, lax.rem(pos + rel, COARSEN))

    def takes(rel):
        return wanted(slot_from(rel), pos)

    def slot_from(rel):
        return lax.rem(pos + COARSEN - rel, COARSEN)

    def fine_load(layer, tap):
        return pltpu.make_async_copy(
            kern_ref.at[layer, tap],
            fine_w.at[layer, :, pl.ds(tap * width, width)],
            load_sem.at[layer, tap],
        )

    def lead_load(tap):
        return pltpu.make_async_copy(
            kern_ref.at[0, tap],
            lead_w.at[pos, :, pl.ds(tap * width, width)],
            lead_sem.at[tap],
        )

    for layer in range(depth):
        for tap in range(TAPS):
            fine_load(layer, tap).start()
    for tap in range(TAPS):
        lead_load(tap).start()

    barrier = pltpu.get_barrier_semaphore()

    def greet(device):
        pl.semaphore_signal(barrier, inc=1, device_id=device, device_id_type=MESH)

    partners = [(has_next, (me + 1, part)), (me > 0, (me - 1, part)),
                (has_group_after, (me + COARSEN, part)), (has_group_before, (me - COARSEN, part)),
                (jnp.logical_and(is_upper, has_group_after), (me + COARSEN - span_low, part)),
                (jnp.logical_and(pos < span_low, has_group_before), (me - COARSEN + span_low, part))]
    for there, device in partners:
        pl.when(there)(lambda device=device: greet(device))
    for rel in range(1, COARSEN):
        greet(peer(rel))
    greet((me, sibling))
    greetings = sum(jnp.where(there, 1, 0) for there, _ in partners)
    pl.semaphore_wait(barrier, COARSEN + greetings)

    def hop(index, source, target):
        return pltpu.make_async_remote_copy(
            src_ref=source, dst_ref=target, send_sem=hop_send.at[index], recv_sem=hop_recv.at[index],
            device_id=(me + 1, part), device_id_type=MESH)

    first_hop = hop(0, guess_ref.at[depth - 1, 0], first_head)
    second_hop = hop(1, corner_out, next_head)
    pl.when(has_next)(first_hop.start)

    def half(which):
        return pl.ds(pl.multiple_of(which * half_rows, 16), half_rows)

    def w_copy(rel):
        return pltpu.make_async_remote_copy(
            src_ref=lead_w.at[pos, half(core)], dst_ref=lead_w.at[pos, half(core)],
            send_sem=w_send.at[rel], recv_sem=w_recv.at[rel],
            device_id=peer(rel), device_id_type=MESH)

    def w_arrival(rel):
        return pltpu.make_async_remote_copy(
            src_ref=lead_w.at[slot_from(rel), half(core)], dst_ref=lead_w.at[slot_from(rel), half(core)],
            send_sem=w_send.at[rel], recv_sem=w_recv.at[rel],
            device_id=peer(rel), device_id_type=MESH)

    def sib_copy(rel, which):
        return pltpu.make_async_remote_copy(
            src_ref=lead_w.at[slot_from(rel), half(which)], dst_ref=lead_w.at[slot_from(rel), half(which)],
            send_sem=sib_send.at[rel], recv_sem=sib_recv.at[rel],
            device_id=(me, sibling), device_id_type=MESH)

    for tap in range(TAPS):
        lead_load(tap).wait()
    early = (None, pos != 1, pos >= 0, pos == COARSEN - 1)
    for rel in (1, 2, 3):
        pl.when(jnp.logical_and(gives(rel), early[rel]))(w_copy(rel).start)

    z_index = lax.broadcasted_iota(jnp.int32, (size_x * size_y, size_z, width), 1)

    def mix(state, weights):
        squashed = jnp.tanh(state).reshape(size_x * size_y, size_z, width)
        below = jnp.where(z_index == 0, 0.0, pltpu.roll(squashed, 1, 1))
        above = jnp.where(z_index == size_z - 1, 0.0, pltpu.roll(squashed, size_z - 1, 1))
        edge = jnp.zeros((size_x, 1, size_z, width), jnp.float32)
        span = size_y * size_z
        for tap_z, shifted in enumerate((below, squashed, above)):
            shifted = shifted.reshape(size_x, size_y, size_z, width)
            even = shifted.reshape(size_x, span, width).astype(jnp.bfloat16)
            odd = jnp.concatenate([edge, shifted, edge], 1)
            odd = odd.reshape(size_x, span + 2 * size_z, width).astype(jnp.bfloat16)
            for tap_y, block in enumerate((odd[:, :span], even, odd[:, 2 * size_z:])):
                column = (tap_y * TAPS + tap_z) * width
                patches[:, :, column:column + width] = block
        left = patches[...].reshape(size_x * span, rows)
        product = jnp.dot(left, weights[...], preferred_element_type=jnp.float32)
        product = product.reshape(size_x, size_y, size_z, TAPS * width)
        plane = jnp.zeros((1, size_y, size_z, width), jnp.float32)
        total = product[..., width:2 * width]
        total = total + jnp.concatenate([plane, product[:-1, :, :, :width]], 0)
        return total + jnp.concatenate([product[1:, :, :, 2 * width:], plane], 0)

    def fine_step(layer):
        state = cur[...]
        mixed = mix(state, fine_w.at[layer])
        return state, mixed, state + fine_size * (mixed + bias_ref[layer])

    pl.when(has_next)(first_hop.wait_send)
    pl.when(me > 0)(first_hop.wait_recv)
    cur[...] = jnp.where(is_first, inputs_ref[...], first_head[...])

    for layer in range(depth):
        for tap in range(TAPS):
            fine_load(layer, tap).wait()

    def sweep_one(layer, carry):
        cur[...] = fine_step(layer)[2]
        return carry

    lax.fori_loop(0, depth, sweep_one, 0)
    corner_out[...] = cur[...]
    pl.when(has_next)(second_hop.start)

    for rel in (1, 2, 3):
        pl.when(jnp.logical_and(gives(rel), jnp.logical_not(early[rel])))(w_copy(rel).start)

    pl.when(has_next)(second_hop.wait_send)
    pl.when(me > 0)(second_hop.wait_recv)

    def head_copy(rel):
        return pltpu.make_async_remote_copy(
            src_ref=next_head, dst_ref=group_in, send_sem=head_send.at[rel], recv_sem=head_recv,
            device_id=peer(rel), device_id_type=MESH)

    leads_group = jnp.logical_and(pos == 0, has_group_before)
    follows = jnp.logical_and(is_upper, has_group_before)
    head[...] = jnp.where(is_first, inputs_ref[...], next_head[...])
    cur[...] = head[...]

    def sweep_two(layer, carry):
        _, mixed, after = fine_step(layer)

        @pl.when(layer == 0)
        def _():
            head_mix[...] = mixed

        cur[...] = after
        return carry

    lax.fori_loop(0, depth, sweep_two, 0)
    defects[pos] = cur[...] - head[...] - coarse_size * head_mix[...]

    def g_copy(rel):
        return pltpu.make_async_remote_copy(
            src_ref=defects.at[pos], dst_ref=defects.at[pos],
            send_sem=g_send.at[rel], recv_sem=g_recv.at[rel], device_id=peer(rel), device_id_type=MESH)

    def g_arrival(rel):
        return pltpu.make_async_remote_copy(
            src_ref=defects.at[slot_from(rel)], dst_ref=defects.at[slot_from(rel)],
            send_sem=g_send.at[rel], recv_sem=g_recv.at[rel], device_id=peer(rel), device_id_type=MESH)

    for rel in range(COARSEN - 1, 0, -1):
        pl.when(gives(rel))(g_copy(rel).start)
    for rel in range(span_low, COARSEN):
        pl.when(leads_group)(head_copy(rel).start)
    for rel in range(1, COARSEN):
        @pl.when(takes(rel))
        def _(rel=rel):
            w_arrival(rel).wait_recv()
            sib_copy(rel, core).start()

    group_in_first = group == 0
    pl.when(follows)(head_copy(1).wait_recv)
    for rel in range(1, COARSEN):
        @pl.when(takes(rel))
        def _(rel=rel):
            sib_copy(rel, 1 - core).wait_recv()
            g_arrival(rel).wait_recv()

    def chain(count):
        def step(turn, carry):
            state = cur[...]
            mixed = mix(state, lead_w.at[turn])

            @pl.when(turn == pos)
            def _():
                head[...] = state
                head_mix[...] = mixed

            after = state + coarse_size * mixed + defects[turn]
            cur[...] = after
            return carry

        lax.fori_loop(0, count, step, 0)

    def jump(index, source, target, back):
        return pltpu.make_async_remote_copy(
            src_ref=source, dst_ref=target, send_sem=jump_send.at[index], recv_sem=jump_recv.at[min(index, 1)],
            device_id=(me + COARSEN - back, part), device_id_type=MESH)

    relaxed = jump(0, corner_out, start_in, 0)
    solved = jump(1, top_out, top_in, 0)
    solved_low = jump(2, top_out, top_in, span_low)
    upper_sends = jnp.logical_and(is_upper, has_group_after)
    is_owner = pos == COARSEN - 1

    @pl.when(is_upper)
    def _():
        cur[...] = jnp.where(group_in_first, inputs_ref[...], group_in[...])
        chain(COARSEN)
        corner_out[...] = cur[...]
        pl.when(upper_sends)(relaxed.start)
        pl.when(follows)(relaxed.wait_recv)
        start = jnp.where(group_in_first, inputs_ref[...], start_in[...])
        top_head[...] = start
        cur[...] = start
        chain(COARSEN)
        top_w = lead_w.at[COARSEN - 1]
        start = top_head[...]
        top_rhs[...] = cur[...] - start - top_size * mix(start, top_w)
        corner = cur[...]
        residual_ref[0, 0] = jnp.where(is_owner, corner - corner_out[...], corner - corner)
        pl.when(follows)(solved.wait_recv)
        top_head[...] = jnp.where(group_in_first, inputs_ref[...], top_in[...])
        top_out[...] = top_head[...] + top_size * mix(top_head[...], top_w) + top_rhs[...]
        pl.when(upper_sends)(solved.start)
        pl.when(upper_sends)(solved_low.start)

    lower_takes = jnp.logical_and(pos < span_low, has_group_before)
    pl.when(lower_takes)(solved_low.wait_recv)

    @pl.when(pos < span_low)
    def _():
        top_head[...] = jnp.where(group_in_first, inputs_ref[...], top_in[...])

    cur[...] = top_head[...]
    chain(pos + 1)

    @pl.when(pos < span_low)
    def _():
        corner = cur[...]
        residual_ref[0, 0] = corner - corner

    first = head[...] + coarse_size * head_mix[...] + defects[pos]
    states_ref[depth - 1, 0] = jnp.where(is_owner, top_out[...], first)
    cur[...] = head[...] + fine_size * (head_mix[...] + bias_ref[0])
    states_ref[0, 0] = cur[...]

    def last_sweep(layer, carry):
        after = fine_step(layer)[2]
        cur[...] = after
        states_ref[layer, 0] = after
        return carry

    lax.fori_loop(1, depth - 1, last_sweep, 0)

    for rel in range(1, COARSEN):
        pl.when(gives(rel))(w_copy(rel).wait_send)
        pl.when(takes(rel))(sib_copy(rel, core).wait_send)
        pl.when(gives(rel))(g_copy(rel).wait_send)
    for rel in range(span_low, COARSEN):
        pl.when(leads_group)(head_copy(rel).wait_send)
    for copy in (relaxed, solved, solved_low):
        pl.when(upper_sends)(copy.wait_send)


def shards(inputs, guess_states, kernels, biases):
    sections = lax.axis_size("layer")
    depth = guess_states.shape[0]
    state = inputs.shape[1:]
    width = state[-1]
    rows = TAPS * TAPS * width
    vmem = pl.BlockSpec(memory_space=pltpu.VMEM)
    anywhere = pl.BlockSpec(memory_space=pl.ANY)
    kernel_rows = kernels.reshape(depth, TAPS, rows, width)
    bias_rows = biases.reshape(depth, 1, 1, width)
    f32_state = pltpu.VMEM(state, jnp.float32)
    dma = pltpu.SemaphoreType.DMA

    def body(*refs):
        cycle_kernel(sections, *refs)

    return tuple(pl.pallas_call(
        body,
        name="mgrit_cycle",
        out_shape=(
            jax.ShapeDtypeStruct(guess_states.shape, jnp.float32),
            jax.ShapeDtypeStruct((1,) + guess_states.shape[1:], jnp.float32),
        ),
        in_specs=[vmem, anywhere, anywhere, vmem],
        out_specs=(vmem, vmem),
        scratch_shapes=[
            pltpu.VMEM((depth, rows, TAPS * width), jnp.bfloat16),
            pltpu.VMEM((COARSEN, rows, TAPS * width), jnp.bfloat16),
            pltpu.VMEM((state[0], state[1] * state[2], rows), jnp.bfloat16),
            f32_state, f32_state, f32_state, f32_state, f32_state, f32_state,
            f32_state, f32_state, f32_state, f32_state,
            pltpu.VMEM((COARSEN,) + state, jnp.float32),
            f32_state, f32_state,
            dma((depth, TAPS)), dma((TAPS,)), dma((2,)), dma((2,)),
            dma((COARSEN,)), dma((COARSEN,)), dma((COARSEN,)), dma((COARSEN,)),
            dma((COARSEN,)), dma, dma((COARSEN,)), dma((COARSEN,)), dma((3,)), dma((2,)),
        ],
        compiler_params=pltpu.CompilerParams(
            collective_id=0, has_side_effects=True, vmem_limit_bytes=60 * 1024 * 1024),
    )(inputs.reshape(state), guess_states, kernel_rows, bias_rows))


def solution(mesh):
    return jax.shard_map(
        shards,
        mesh=mesh,
        in_specs=(
            P("batch", None, None, None, None),
            P("layer", "batch", None, None, None, None),
            P("layer", None, None, None, None, None),
            P("layer", None),
        ),
        out_specs=(
            P("layer", "batch", None, None, None, None),
            P("layer", "batch", None, None, None, None),
        ),
        check_vma=False,
    )
```

```python
import jax
import jax.numpy as jnp
from jax import lax
from jax.experimental import pallas as pl
from jax.experimental.pallas import tpu as pltpu
from jax.sharding import PartitionSpec as P

COARSEN = 4
TAPS = 3
MESH = pl.DeviceIdType.MESH


def cycle_kernel(sections, inputs_hbm, guess_ref, kern_ref, bias_hbm, states_ref, residual_ref,
                 inputs_ref, bias_ref,
                 fine_w, lead_w, patches, cur, head, head_mix, first_head, next_head, corner_out,
                 start_in, group_in, top_head, top_rhs, defects, top_in, top_out,
                 load_sem, lead_sem, small_sem, hop_send, hop_recv, w_send, w_recv, sib_send, sib_recv,
                 head_send, head_recv, g_send, g_recv, jump_send, jump_recv):
    depth = guess_ref.shape[0]
    size_x, size_y, size_z, width = inputs_ref.shape
    groups = sections // COARSEN
    fine_size = 2.0 / (depth * sections)
    coarse_size = depth * fine_size
    top_size = COARSEN * coarse_size
    rows = TAPS * TAPS * width
    half_rows = rows // 2
    me = lax.axis_index("layer")
    part = lax.axis_index("batch")
    pos = lax.rem(me, COARSEN)
    group = me // COARSEN
    core = lax.rem(part, 2)
    sibling = part + 1 - 2 * core
    is_first = me == 0
    has_next = me < sections - 1
    has_group_before = group > 0
    has_group_after = group < groups - 1
    span_low = COARSEN // 2
    is_upper = pos >= span_low

    def peer(rel):
        return (group * COARSEN + lax.rem(pos + rel, COARSEN), part)

    def wanted(source, target):
        return jnp.logical_or(target >= span_low, target > source)

    def gives(rel):
        return wanted(pos, lax.rem(pos + rel, COARSEN))

    def takes(rel):
        return wanted(slot_from(rel), pos)

    def slot_from(rel):
        return lax.rem(pos + COARSEN - rel, COARSEN)

    def fine_load(layer, tap):
        return pltpu.make_async_copy(
            kern_ref.at[layer, tap],
            fine_w.at[layer, :, pl.ds(tap * width, width)],
            load_sem.at[layer, tap],
        )

    def lead_load(tap):
        return pltpu.make_async_copy(
            kern_ref.at[0, tap],
            lead_w.at[pos, :, pl.ds(tap * width, width)],
            lead_sem.at[tap],
        )

    inputs_load = pltpu.make_async_copy(inputs_hbm, inputs_ref, small_sem.at[0])
    bias_load = pltpu.make_async_copy(bias_hbm, bias_ref, small_sem.at[1])
    for tap in range(TAPS):
        lead_load(tap).start()
    inputs_load.start()
    bias_load.start()
    for layer in range(depth):
        for tap in range(TAPS):
            fine_load(layer, tap).start()

    barrier = pltpu.get_barrier_semaphore()

    def greet(device):
        pl.semaphore_signal(barrier, inc=1, device_id=device, device_id_type=MESH)

    partners = [(has_next, (me + 1, part)), (me > 0, (me - 1, part)),
                (has_group_after, (me + COARSEN, part)), (has_group_before, (me - COARSEN, part)),
                (jnp.logical_and(is_upper, has_group_after), (me + COARSEN - span_low, part)),
                (jnp.logical_and(pos < span_low, has_group_before), (me - COARSEN + span_low, part))]
    for there, device in partners:
        pl.when(there)(lambda device=device: greet(device))
    for rel in range(1, COARSEN):
        greet(peer(rel))
    greet((me, sibling))
    greetings = sum(jnp.where(there, 1, 0) for there, _ in partners)
    pl.semaphore_wait(barrier, COARSEN + greetings)

    def hop(index, source, target):
        return pltpu.make_async_remote_copy(
            src_ref=source, dst_ref=target, send_sem=hop_send.at[index], recv_sem=hop_recv.at[index],
            device_id=(me + 1, part), device_id_type=MESH)

    first_hop = hop(0, guess_ref.at[depth - 1, 0], first_head)
    second_hop = hop(1, corner_out, next_head)
    pl.when(has_next)(first_hop.start)

    def half(which):
        return pl.ds(pl.multiple_of(which * half_rows, 16), half_rows)

    def w_copy(rel):
        return pltpu.make_async_remote_copy(
            src_ref=lead_w.at[pos, half(core)], dst_ref=lead_w.at[pos, half(core)],
            send_sem=w_send.at[rel], recv_sem=w_recv.at[rel],
            device_id=peer(rel), device_id_type=MESH)

    def w_arrival(rel):
        return pltpu.make_async_remote_copy(
            src_ref=lead_w.at[slot_from(rel), half(core)], dst_ref=lead_w.at[slot_from(rel), half(core)],
            send_sem=w_send.at[rel], recv_sem=w_recv.at[rel],
            device_id=peer(rel), device_id_type=MESH)

    def sib_copy(rel, which):
        return pltpu.make_async_remote_copy(
            src_ref=lead_w.at[slot_from(rel), half(which)], dst_ref=lead_w.at[slot_from(rel), half(which)],
            send_sem=sib_send.at[rel], recv_sem=sib_recv.at[rel],
            device_id=(me, sibling), device_id_type=MESH)

    for tap in range(TAPS):
        lead_load(tap).wait()
    early = (None, pos != 1, pos >= 0, pos == COARSEN - 1)
    for rel in (1, 2, 3):
        pl.when(jnp.logical_and(gives(rel), early[rel]))(w_copy(rel).start)

    z_index = lax.broadcasted_iota(jnp.int32, (size_x * size_y, size_z, width), 1)

    def mix(state, weights):
        squashed = jnp.tanh(state).reshape(size_x * size_y, size_z, width)
        below = jnp.where(z_index == 0, 0.0, pltpu.roll(squashed, 1, 1))
        above = jnp.where(z_index == size_z - 1, 0.0, pltpu.roll(squashed, size_z - 1, 1))
        span = size_y * size_z
        edge = jnp.zeros((size_x, size_z, width), jnp.float32)
        for tap_z, shifted in enumerate((below, squashed, above)):
            shifted = shifted.reshape(size_x, span, width)
            even = shifted.astype(jnp.bfloat16)
            odd = jnp.concatenate([edge, shifted, edge], 1).astype(jnp.bfloat16)
            for tap_y, block in enumerate((odd[:, :span], even, odd[:, 2 * size_z:])):
                column = (tap_y * TAPS + tap_z) * width
                patches[:, :, column:column + width] = block
        left = patches[...].reshape(size_x * span, rows)
        product = jnp.dot(left, weights[...], preferred_element_type=jnp.float32)
        product = product.reshape(size_x, size_y, size_z, TAPS * width)
        plane = jnp.zeros((1, size_y, size_z, width), jnp.float32)
        total = product[..., width:2 * width]
        total = total + jnp.concatenate([plane, product[:-1, :, :, :width]], 0)
        return total + jnp.concatenate([product[1:, :, :, 2 * width:], plane], 0)

    def fine_step(layer):
        state = cur[...]
        mixed = mix(state, fine_w.at[layer])
        return state, mixed, state + fine_size * (mixed + bias_ref[layer])

    pl.when(has_next)(first_hop.wait_send)
    pl.when(me > 0)(first_hop.wait_recv)
    inputs_load.wait()
    bias_load.wait()
    cur[...] = jnp.where(is_first, inputs_ref[...], first_head[...])

    for layer in range(depth):
        for tap in range(TAPS):
            fine_load(layer, tap).wait()

    def sweep_one(layer, carry):
        cur[...] = fine_step(layer)[2]
        return carry

    lax.fori_loop(0, depth, sweep_one, 0)
    corner_out[...] = cur[...]
    pl.when(has_next)(second_hop.start)

    for rel in (1, 2, 3):
        pl.when(jnp.logical_and(gives(rel), jnp.logical_not(early[rel])))(w_copy(rel).start)

    pl.when(has_next)(second_hop.wait_send)
    pl.when(me > 0)(second_hop.wait_recv)

    def head_copy(rel):
        return pltpu.make_async_remote_copy(
            src_ref=next_head, dst_ref=group_in, send_sem=head_send.at[rel], recv_sem=head_recv,
            device_id=peer(rel), device_id_type=MESH)

    leads_group = jnp.logical_and(pos == 0, has_group_before)
    follows = jnp.logical_and(is_upper, has_group_before)
    head[...] = jnp.where(is_first, inputs_ref[...], next_head[...])
    cur[...] = head[...]

    def sweep_two(layer, carry):
        _, mixed, after = fine_step(layer)

        @pl.when(layer == 0)
        def _():
            head_mix[...] = mixed

        cur[...] = after
        return carry

    lax.fori_loop(0, depth, sweep_two, 0)
    defects[pos] = cur[...] - head[...] - coarse_size * head_mix[...]

    def g_copy(rel):
        return pltpu.make_async_remote_copy(
            src_ref=defects.at[pos], dst_ref=defects.at[pos],
            send_sem=g_send.at[rel], recv_sem=g_recv.at[rel], device_id=peer(rel), device_id_type=MESH)

    def g_arrival(rel):
        return pltpu.make_async_remote_copy(
            src_ref=defects.at[slot_from(rel)], dst_ref=defects.at[slot_from(rel)],
            send_sem=g_send.at[rel], recv_sem=g_recv.at[rel], device_id=peer(rel), device_id_type=MESH)

    for rel in range(COARSEN - 1, 0, -1):
        pl.when(gives(rel))(g_copy(rel).start)
    for rel in range(span_low, COARSEN):
        pl.when(leads_group)(head_copy(rel).start)
    for rel in range(1, COARSEN):
        @pl.when(takes(rel))
        def _(rel=rel):
            w_arrival(rel).wait_recv()
            sib_copy(rel, core).start()

    group_in_first = group == 0
    pl.when(follows)(head_copy(1).wait_recv)
    for rel in range(1, COARSEN):
        @pl.when(takes(rel))
        def _(rel=rel):
            sib_copy(rel, 1 - core).wait_recv()
            g_arrival(rel).wait_recv()

    def chain(count):
        def step(turn, carry):
            state = cur[...]
            mixed = mix(state, lead_w.at[turn])

            @pl.when(turn == pos)
            def _():
                head[...] = state
                head_mix[...] = mixed

            after = state + coarse_size * mixed + defects[turn]
            cur[...] = after
            return carry

        lax.fori_loop(0, count, step, 0)

    def jump(index, source, target, back):
        return pltpu.make_async_remote_copy(
            src_ref=source, dst_ref=target, send_sem=jump_send.at[index], recv_sem=jump_recv.at[min(index, 1)],
            device_id=(me + COARSEN - back, part), device_id_type=MESH)

    relaxed = jump(0, corner_out, start_in, 0)
    solved = jump(1, top_out, top_in, 0)
    solved_low = jump(2, top_out, top_in, span_low)
    upper_sends = jnp.logical_and(is_upper, has_group_after)
    is_owner = pos == COARSEN - 1

    @pl.when(is_upper)
    def _():
        cur[...] = jnp.where(group_in_first, inputs_ref[...], group_in[...])
        chain(COARSEN)
        corner_out[...] = cur[...]
        pl.when(upper_sends)(relaxed.start)
        pl.when(follows)(relaxed.wait_recv)
        start = jnp.where(group_in_first, inputs_ref[...], start_in[...])
        top_head[...] = start

        @pl.when(has_group_before)
        def _():
            cur[...] = start_in[...]
            chain(COARSEN)

        top_w = lead_w.at[COARSEN - 1]
        start = top_head[...]
        top_rhs[...] = cur[...] - start - top_size * mix(start, top_w)
        corner = cur[...]
        residual_ref[0, 0] = jnp.where(is_owner, corner - corner_out[...], corner - corner)
        pl.when(follows)(solved.wait_recv)
        top_head[...] = jnp.where(group_in_first, inputs_ref[...], top_in[...])
        top_out[...] = top_head[...] + top_size * mix(top_head[...], top_w) + top_rhs[...]
        pl.when(upper_sends)(solved.start)
        pl.when(upper_sends)(solved_low.start)

    lower_takes = jnp.logical_and(pos < span_low, has_group_before)
    pl.when(lower_takes)(solved_low.wait_recv)

    @pl.when(pos < span_low)
    def _():
        top_head[...] = jnp.where(group_in_first, inputs_ref[...], top_in[...])

    cur[...] = top_head[...]
    chain(pos + 1)

    @pl.when(pos < span_low)
    def _():
        corner = cur[...]
        residual_ref[0, 0] = corner - corner

    first = head[...] + coarse_size * head_mix[...] + defects[pos]
    states_ref[depth - 1, 0] = jnp.where(is_owner, top_out[...], first)
    cur[...] = head[...] + fine_size * (head_mix[...] + bias_ref[0])
    states_ref[0, 0] = cur[...]

    def last_sweep(layer, carry):
        after = fine_step(layer)[2]
        cur[...] = after
        states_ref[layer, 0] = after
        return carry

    lax.fori_loop(1, depth - 1, last_sweep, 0)

    for rel in range(1, COARSEN):
        pl.when(gives(rel))(w_copy(rel).wait_send)
        pl.when(takes(rel))(sib_copy(rel, core).wait_send)
        pl.when(gives(rel))(g_copy(rel).wait_send)
    for rel in range(span_low, COARSEN):
        pl.when(leads_group)(head_copy(rel).wait_send)
    for copy in (relaxed, solved, solved_low):
        pl.when(upper_sends)(copy.wait_send)


def shards(inputs, guess_states, kernels, biases):
    sections = lax.axis_size("layer")
    depth = guess_states.shape[0]
    state = inputs.shape[1:]
    width = state[-1]
    rows = TAPS * TAPS * width
    vmem = pl.BlockSpec(memory_space=pltpu.VMEM)
    hbm = pl.BlockSpec(memory_space=pltpu.HBM)
    kernel_rows = kernels.reshape(depth, TAPS, rows, width)
    bias_rows = biases.reshape(depth, 1, 1, width)
    f32_state = pltpu.VMEM(state, jnp.float32)
    dma = pltpu.SemaphoreType.DMA

    def body(*refs):
        cycle_kernel(sections, *refs)

    return tuple(pl.pallas_call(
        body,
        name="mgrit_cycle",
        out_shape=(
            jax.ShapeDtypeStruct(guess_states.shape, jnp.float32),
            jax.ShapeDtypeStruct((1,) + guess_states.shape[1:], jnp.float32),
        ),
        in_specs=[hbm, hbm, hbm, hbm],
        out_specs=(vmem, vmem),
        scratch_shapes=[
            f32_state, pltpu.VMEM(bias_rows.shape, jnp.float32),
            pltpu.VMEM((depth, rows, TAPS * width), jnp.bfloat16),
            pltpu.VMEM((COARSEN, rows, TAPS * width), jnp.bfloat16),
            pltpu.VMEM((state[0], state[1] * state[2], rows), jnp.bfloat16),
            f32_state, f32_state, f32_state, f32_state, f32_state, f32_state,
            f32_state, f32_state, f32_state, f32_state,
            pltpu.VMEM((COARSEN,) + state, jnp.float32),
            f32_state, f32_state,
            dma((depth, TAPS)), dma((TAPS,)), dma((2,)), dma((2,)), dma((2,)),
            dma((COARSEN,)), dma((COARSEN,)), dma((COARSEN,)), dma((COARSEN,)),
            dma((COARSEN,)), dma, dma((COARSEN,)), dma((COARSEN,)), dma((3,)), dma((2,)),
        ],
        compiler_params=pltpu.CompilerParams(
            collective_id=0, has_side_effects=True, vmem_limit_bytes=60 * 1024 * 1024),
    )(inputs.reshape(state), guess_states, kernel_rows, bias_rows))


def solution(mesh):
    return jax.shard_map(
        shards,
        mesh=mesh,
        in_specs=(
            P("batch", None, None, None, None),
            P("layer", "batch", None, None, None, None),
            P("layer", None, None, None, None, None),
            P("layer", None),
        ),
        out_specs=(
            P("layer", "batch", None, None, None, None),
            P("layer", "batch", None, None, None, None),
        ),
        check_vma=False,
    )
```

```python
import jax
import jax.numpy as jnp
from jax import lax
from jax.experimental import pallas as pl
from jax.experimental.pallas import tpu as pltpu
from jax.sharding import PartitionSpec as P

COARSEN = 4
TAPS = 3
MESH = pl.DeviceIdType.MESH


def cycle_kernel(sections, inputs_hbm, guess_ref, kern_ref, bias_hbm, states_ref, residual_ref,
                 inputs_ref, bias_ref,
                 fine_w, lead_w, patches, cur, head, head_mix, first_head, next_head, corner_out,
                 start_in, group_in, top_head, top_rhs, defects, top_in, top_out,
                 load_sem, lead_sem, small_sem, hop_send, hop_recv, w_send, w_recv, sib_send, sib_recv,
                 head_send, head_recv, g_send, g_recv, jump_send, jump_recv):
    depth = guess_ref.shape[0]
    size_x, size_y, size_z, width = inputs_ref.shape
    groups = sections // COARSEN
    fine_size = 2.0 / (depth * sections)
    coarse_size = depth * fine_size
    top_size = COARSEN * coarse_size
    rows = TAPS * TAPS * width
    half_rows = rows // 2
    me = lax.axis_index("layer")
    part = lax.axis_index("batch")
    pos = lax.rem(me, COARSEN)
    group = me // COARSEN
    core = lax.rem(part, 2)
    sibling = part + 1 - 2 * core
    is_first = me == 0
    has_next = me < sections - 1
    has_group_before = group > 0
    has_group_after = group < groups - 1
    span_low = COARSEN // 2
    is_upper = pos >= span_low

    def peer(rel):
        return (group * COARSEN + lax.rem(pos + rel, COARSEN), part)

    def wanted(source, target):
        return jnp.logical_or(target >= span_low, target > source)

    def gives(rel):
        return wanted(pos, lax.rem(pos + rel, COARSEN))

    def takes(rel):
        return wanted(slot_from(rel), pos)

    def slot_from(rel):
        return lax.rem(pos + COARSEN - rel, COARSEN)

    def fine_load(layer, tap):
        return pltpu.make_async_copy(
            kern_ref.at[layer, tap],
            fine_w.at[layer, :, pl.ds(tap * width, width)],
            load_sem.at[layer, tap],
        )

    def lead_load(tap):
        return pltpu.make_async_copy(
            kern_ref.at[0, tap],
            lead_w.at[pos, :, pl.ds(tap * width, width)],
            lead_sem.at[tap],
        )

    inputs_load = pltpu.make_async_copy(inputs_hbm, inputs_ref, small_sem.at[0])
    bias_load = pltpu.make_async_copy(bias_hbm, bias_ref, small_sem.at[1])
    for tap in range(TAPS):
        lead_load(tap).start()
    inputs_load.start()
    bias_load.start()
    for layer in range(depth):
        for tap in range(TAPS):
            fine_load(layer, tap).start()

    barrier = pltpu.get_barrier_semaphore()

    def greet(device):
        pl.semaphore_signal(barrier, inc=1, device_id=device, device_id_type=MESH)

    partners = [(has_next, (me + 1, part)), (me > 0, (me - 1, part)),
                (has_group_after, (me + COARSEN, part)), (has_group_before, (me - COARSEN, part)),
                (jnp.logical_and(is_upper, has_group_after), (me + COARSEN - span_low, part)),
                (jnp.logical_and(pos < span_low, has_group_before), (me - COARSEN + span_low, part))]
    for there, device in partners:
        pl.when(there)(lambda device=device: greet(device))
    for rel in range(1, COARSEN):
        greet(peer(rel))
    greet((me, sibling))
    greetings = sum(jnp.where(there, 1, 0) for there, _ in partners)
    pl.semaphore_wait(barrier, COARSEN + greetings)

    def hop(index, source, target):
        return pltpu.make_async_remote_copy(
            src_ref=source, dst_ref=target, send_sem=hop_send.at[index], recv_sem=hop_recv.at[index],
            device_id=(me + 1, part), device_id_type=MESH)

    first_hop = hop(0, guess_ref.at[depth - 1, 0], first_head)
    second_hop = hop(1, corner_out, next_head)
    pl.when(has_next)(first_hop.start)

    def half(which):
        return pl.ds(pl.multiple_of(which * half_rows, 16), half_rows)

    def w_copy(rel):
        return pltpu.make_async_remote_copy(
            src_ref=lead_w.at[pos, half(core)], dst_ref=lead_w.at[pos, half(core)],
            send_sem=w_send.at[rel], recv_sem=w_recv.at[rel],
            device_id=peer(rel), device_id_type=MESH)

    def w_arrival(rel):
        return pltpu.make_async_remote_copy(
            src_ref=lead_w.at[slot_from(rel), half(core)], dst_ref=lead_w.at[slot_from(rel), half(core)],
            send_sem=w_send.at[rel], recv_sem=w_recv.at[rel],
            device_id=peer(rel), device_id_type=MESH)

    def sib_copy(rel, which):
        return pltpu.make_async_remote_copy(
            src_ref=lead_w.at[slot_from(rel), half(which)], dst_ref=lead_w.at[slot_from(rel), half(which)],
            send_sem=sib_send.at[rel], recv_sem=sib_recv.at[rel],
            device_id=(me, sibling), device_id_type=MESH)

    for tap in range(TAPS):
        lead_load(tap).wait()
    early = (None, pos != 1, pos >= 0, pos == COARSEN - 1)
    for rel in (1, 2, 3):
        pl.when(jnp.logical_and(gives(rel), early[rel]))(w_copy(rel).start)

    z_index = lax.broadcasted_iota(jnp.int32, (size_x * size_y, size_z, width), 1)

    def mix(state, weights):
        squashed = jnp.tanh(state).reshape(size_x * size_y, size_z, width)
        below = jnp.where(z_index == 0, 0.0, pltpu.roll(squashed, 1, 1))
        above = jnp.where(z_index == size_z - 1, 0.0, pltpu.roll(squashed, size_z - 1, 1))
        span = size_y * size_z
        edge = jnp.zeros((size_x, size_z, width), jnp.float32)
        for tap_z, shifted in enumerate((below, squashed, above)):
            shifted = shifted.reshape(size_x, span, width)
            even = shifted.astype(jnp.bfloat16)
            odd = jnp.concatenate([edge, shifted, edge], 1).astype(jnp.bfloat16)
            for tap_y, block in enumerate((odd[:, :span], even, odd[:, 2 * size_z:])):
                column = (tap_y * TAPS + tap_z) * width
                patches[:, :, column:column + width] = block
        left = patches[...].reshape(size_x * span, rows)
        product = jnp.dot(left, weights[...], preferred_element_type=jnp.float32)
        product = product.reshape(size_x, size_y, size_z, TAPS * width)
        plane = jnp.zeros((1, size_y, size_z, width), jnp.float32)
        total = product[..., width:2 * width]
        total = total + jnp.concatenate([plane, product[:-1, :, :, :width]], 0)
        return total + jnp.concatenate([product[1:, :, :, 2 * width:], plane], 0)

    def fine_step(layer):
        state = cur[...]
        mixed = mix(state, fine_w.at[layer])
        return state, mixed, state + fine_size * (mixed + bias_ref[layer])

    pl.when(has_next)(first_hop.wait_send)
    pl.when(me > 0)(first_hop.wait_recv)
    inputs_load.wait()
    bias_load.wait()
    cur[...] = jnp.where(is_first, inputs_ref[...], first_head[...])

    for layer in range(depth):
        for tap in range(TAPS):
            fine_load(layer, tap).wait()

    def sweep_one(layer, carry):
        cur[...] = fine_step(layer)[2]
        return carry

    lax.fori_loop(0, depth, sweep_one, 0)
    corner_out[...] = cur[...]
    pl.when(has_next)(second_hop.start)

    for rel in (1, 2, 3):
        pl.when(jnp.logical_and(gives(rel), jnp.logical_not(early[rel])))(w_copy(rel).start)

    pl.when(has_next)(second_hop.wait_send)
    pl.when(me > 0)(second_hop.wait_recv)

    def head_copy(rel):
        return pltpu.make_async_remote_copy(
            src_ref=next_head, dst_ref=group_in, send_sem=head_send.at[rel], recv_sem=head_recv,
            device_id=peer(rel), device_id_type=MESH)

    leads_group = jnp.logical_and(pos == 0, has_group_before)
    follows = jnp.logical_and(is_upper, has_group_before)
    head[...] = jnp.where(is_first, inputs_ref[...], next_head[...])
    cur[...] = head[...]

    def sweep_two(layer, carry):
        _, mixed, after = fine_step(layer)

        @pl.when(layer == 0)
        def _():
            head_mix[...] = mixed

        cur[...] = after
        return carry

    lax.fori_loop(0, depth, sweep_two, 0)
    defects[pos] = cur[...] - head[...] - coarse_size * head_mix[...]

    def g_copy(rel):
        return pltpu.make_async_remote_copy(
            src_ref=defects.at[pos], dst_ref=defects.at[pos],
            send_sem=g_send.at[rel], recv_sem=g_recv.at[rel], device_id=peer(rel), device_id_type=MESH)

    def g_arrival(rel):
        return pltpu.make_async_remote_copy(
            src_ref=defects.at[slot_from(rel)], dst_ref=defects.at[slot_from(rel)],
            send_sem=g_send.at[rel], recv_sem=g_recv.at[rel], device_id=peer(rel), device_id_type=MESH)

    for rel in range(COARSEN - 1, 0, -1):
        pl.when(gives(rel))(g_copy(rel).start)
    for rel in range(span_low, COARSEN):
        pl.when(leads_group)(head_copy(rel).start)
    for rel in range(1, COARSEN):
        @pl.when(takes(rel))
        def _(rel=rel):
            w_arrival(rel).wait_recv()
            sib_copy(rel, core).start()

    group_in_first = group == 0
    pl.when(follows)(head_copy(1).wait_recv)
    for rel in range(1, COARSEN):
        @pl.when(takes(rel))
        def _(rel=rel):
            sib_copy(rel, 1 - core).wait_recv()

        @pl.when(jnp.logical_and(takes(rel), pos < span_low))
        def _(rel=rel):
            g_arrival(rel).wait_recv()

    def chain(count, arriving=False):
        def step(turn, carry):
            state = cur[...]
            mixed = mix(state, lead_w.at[turn])

            @pl.when(turn == pos)
            def _():
                head[...] = state
                head_mix[...] = mixed

            if arriving:
                rel = lax.rem(pos + COARSEN - turn, COARSEN)
                pl.when(rel > 0)(g_arrival(rel).wait_recv)
            after = state + coarse_size * mixed + defects[turn]
            cur[...] = after
            return carry

        lax.fori_loop(0, count, step, 0)

    def jump(index, source, target, back):
        return pltpu.make_async_remote_copy(
            src_ref=source, dst_ref=target, send_sem=jump_send.at[index], recv_sem=jump_recv.at[min(index, 1)],
            device_id=(me + COARSEN - back, part), device_id_type=MESH)

    relaxed = jump(0, corner_out, start_in, 0)
    solved = jump(1, top_out, top_in, 0)
    solved_low = jump(2, top_out, top_in, span_low)
    upper_sends = jnp.logical_and(is_upper, has_group_after)
    is_owner = pos == COARSEN - 1

    @pl.when(is_upper)
    def _():
        cur[...] = jnp.where(group_in_first, inputs_ref[...], group_in[...])
        chain(COARSEN, arriving=True)
        corner_out[...] = cur[...]
        pl.when(upper_sends)(relaxed.start)
        pl.when(follows)(relaxed.wait_recv)
        start = jnp.where(group_in_first, inputs_ref[...], start_in[...])
        top_head[...] = start

        @pl.when(has_group_before)
        def _():
            cur[...] = start_in[...]
            chain(COARSEN)

        top_w = lead_w.at[COARSEN - 1]
        start = top_head[...]
        top_rhs[...] = cur[...] - start - top_size * mix(start, top_w)
        corner = cur[...]
        residual_ref[0, 0] = jnp.where(is_owner, corner - corner_out[...], corner - corner)
        pl.when(follows)(solved.wait_recv)
        top_head[...] = jnp.where(group_in_first, inputs_ref[...], top_in[...])
        top_out[...] = top_head[...] + top_size * mix(top_head[...], top_w) + top_rhs[...]
        pl.when(upper_sends)(solved.start)
        pl.when(upper_sends)(solved_low.start)

    lower_takes = jnp.logical_and(pos < span_low, has_group_before)
    pl.when(lower_takes)(solved_low.wait_recv)

    @pl.when(pos < span_low)
    def _():
        top_head[...] = jnp.where(group_in_first, inputs_ref[...], top_in[...])

    cur[...] = top_head[...]
    chain(pos + 1)

    @pl.when(pos < span_low)
    def _():
        corner = cur[...]
        residual_ref[0, 0] = corner - corner

    first = head[...] + coarse_size * head_mix[...] + defects[pos]
    states_ref[depth - 1, 0] = jnp.where(is_owner, top_out[...], first)
    cur[...] = head[...] + fine_size * (head_mix[...] + bias_ref[0])
    states_ref[0, 0] = cur[...]

    def last_sweep(layer, carry):
        after = fine_step(layer)[2]
        cur[...] = after
        states_ref[layer, 0] = after
        return carry

    lax.fori_loop(1, depth - 1, last_sweep, 0)

    for rel in range(1, COARSEN):
        pl.when(gives(rel))(w_copy(rel).wait_send)
        pl.when(takes(rel))(sib_copy(rel, core).wait_send)
        pl.when(gives(rel))(g_copy(rel).wait_send)
    for rel in range(span_low, COARSEN):
        pl.when(leads_group)(head_copy(rel).wait_send)
    for copy in (relaxed, solved, solved_low):
        pl.when(upper_sends)(copy.wait_send)


def shards(inputs, guess_states, kernels, biases):
    sections = lax.axis_size("layer")
    depth = guess_states.shape[0]
    state = inputs.shape[1:]
    width = state[-1]
    rows = TAPS * TAPS * width
    vmem = pl.BlockSpec(memory_space=pltpu.VMEM)
    hbm = pl.BlockSpec(memory_space=pltpu.HBM)
    kernel_rows = kernels.reshape(depth, TAPS, rows, width)
    bias_rows = biases.reshape(depth, 1, 1, width)
    f32_state = pltpu.VMEM(state, jnp.float32)
    dma = pltpu.SemaphoreType.DMA

    def body(*refs):
        cycle_kernel(sections, *refs)

    return tuple(pl.pallas_call(
        body,
        name="mgrit_cycle",
        out_shape=(
            jax.ShapeDtypeStruct(guess_states.shape, jnp.float32),
            jax.ShapeDtypeStruct((1,) + guess_states.shape[1:], jnp.float32),
        ),
        in_specs=[hbm, hbm, hbm, hbm],
        out_specs=(vmem, vmem),
        scratch_shapes=[
            f32_state, pltpu.VMEM(bias_rows.shape, jnp.float32),
            pltpu.VMEM((depth, rows, TAPS * width), jnp.bfloat16),
            pltpu.VMEM((COARSEN, rows, TAPS * width), jnp.bfloat16),
            pltpu.VMEM((state[0], state[1] * state[2], rows), jnp.bfloat16),
            f32_state, f32_state, f32_state, f32_state, f32_state, f32_state,
            f32_state, f32_state, f32_state, f32_state,
            pltpu.VMEM((COARSEN,) + state, jnp.float32),
            f32_state, f32_state,
            dma((depth, TAPS)), dma((TAPS,)), dma((2,)), dma((2,)), dma((2,)),
            dma((COARSEN,)), dma((COARSEN,)), dma((COARSEN,)), dma((COARSEN,)),
            dma((COARSEN,)), dma, dma((COARSEN,)), dma((COARSEN,)), dma((3,)), dma((2,)),
        ],
        compiler_params=pltpu.CompilerParams(
            collective_id=0, has_side_effects=True, vmem_limit_bytes=60 * 1024 * 1024),
    )(inputs.reshape(state), guess_states, kernel_rows, bias_rows))


def solution(mesh):
    return jax.shard_map(
        shards,
        mesh=mesh,
        in_specs=(
            P("batch", None, None, None, None),
            P("layer", "batch", None, None, None, None),
            P("layer", None, None, None, None, None),
            P("layer", None),
        ),
        out_specs=(
            P("layer", "batch", None, None, None, None),
            P("layer", "batch", None, None, None, None),
        ),
        check_vma=False,
    )
```
